32 devices in a mesh: section: 2 (over y), blk: 8 (over z, x), mp: 2 (over core).
Axes of the slice: x: 2, y: 2, z: 4, core: 2. Of those that a mesh axis runs over, the one named last changes fastest.
Arguments:
- queries: bfloat16 [2, 1024, 4096], P('section', 'blk', 'mp'), may hold values from -210 to 210
- encoder_states: bfloat16 [512, 2048], P(('blk', 'section', 'mp')), may hold values from -200 to 200
- norm_gain: float32 [2048], replicated, may hold values from 0.25 to 1.75
- kv_weight: bfloat16 [2, 2048, 2, 512], P('section', 'blk', None, 'mp'), may hold values from -0.125 to 0.125
- span_len: int32 [64], replicated, may hold values from 1 to 57, as said below
- span_owner: int32 [64], replicated, may hold values from 0 to 7, as said below
Outputs:
- attended: bfloat16 [2, 1024, 4096], P('section', 'blk', 'mp')
The draws below stay inside these ranges and needn't reach their ends.
Inputs may be any that keep to these rules, and one draw needn't show every extreme that they name: `span_owner`: each span lies whole in the slots of one blk index; each blk index owns exactly 8 spans. `span_len`: the spans of one blk index hold at most 64 tokens together, exactly 64 for some blk index in every draw; all spans hold 288 tokens together; one span holds exactly 57 tokens in every draw.
All inputs are finite; a program needn't handle non-finite values.
Results may differ from the reference program's by a relative error of at most 0.0094.
Values may be sent and summed in bfloat16 or wider, within the bound.
No kernel may reach another device: no remote copies, remote signals or barrier semaphores. Data moves between devices by JAX's collectives and lax.ppermute only.
A program may use at most 64 MiB of HBM per device.

```python
import math
import jax
import jax.numpy as jnp
from jax import lax

DE = 2048
HEADS = 32
KVH = 4
HD = 128
MEAN = 36
CPD = 8
CAP = 64
SLOTS = 512
QTOK = 1024
SPANS = 64
N_SECTION = 2
N_BLK = 8


def draw_queries(key, part):
    shape = (N_SECTION, QTOK, HEADS * HD)
    return (jnp.clip(jax.random.normal(key, shape, jnp.float32), -6.0, 6.0) * 2.5).astype(jnp.bfloat16)


def draw_encoder_states(key, part):
    first_key, second_key, third_key = jax.random.split(key, 3)
    row_scale = jnp.exp(jax.random.uniform(second_key, (SLOTS, 1), jnp.float32, 0.0, math.log(10.0)))
    column_scale = jnp.exp(jax.random.uniform(third_key, (1, DE), jnp.float32, 0.0, math.log(4.0)))
    base = jnp.clip(jax.random.normal(first_key, (SLOTS, DE), jnp.float32), -5.0, 5.0)
    return (base * row_scale * column_scale).astype(jnp.bfloat16)


def span_plan(key):
    base_key = jax.random.fold_in(key, 7)
    first_key, second_key, third_key, fourth_key = jax.random.split(base_key, 4)
    order = jax.random.permutation(first_key, N_BLK)
    half_count = N_BLK // 2
    offsets = jax.random.randint(second_key, (half_count,), 0, MEAN - CPD + 1)
    offsets = offsets.at[0].set(MEAN - CPD)
    paired = jnp.concatenate([MEAN + offsets, MEAN - offsets]).astype(jnp.int32)
    device_load = jnp.zeros((N_BLK,), jnp.int32).at[order].set(paired)
    cut_points = jax.random.randint(third_key, (N_BLK, CPD - 1), 0, (device_load - CPD + 1)[:, None])
    cut_points = jnp.sort(cut_points, axis=1)
    fullest = (jnp.arange(N_BLK, dtype=jnp.int32) == order[0])[:, None]
    cut_points = jnp.where(fullest, 0, cut_points)
    edges = jnp.concatenate([jnp.zeros((N_BLK, 1), jnp.int32), cut_points.astype(jnp.int32), (device_load - CPD)[:, None]], axis=1)
    lengths = edges[:, 1:] - edges[:, :-1] + 1
    owners = jnp.broadcast_to(jnp.arange(N_BLK, dtype=jnp.int32)[:, None], (N_BLK, CPD))
    shuffle = jax.random.permutation(fourth_key, SPANS)
    span_len = jnp.zeros((SPANS,), jnp.int32).at[shuffle].set(lengths.reshape(-1).astype(jnp.int32))
    span_owner = jnp.zeros((SPANS,), jnp.int32).at[shuffle].set(owners.reshape(-1))
    return (span_len, span_owner)


def draw_span_len(key, part):
    return span_plan(key)[0]


def draw_span_owner(key, part):
    return span_plan(key)[1]


def block_levels(key, dims, cuts, smallest, high):
    factor_of, own = 1.0, jax.random.fold_in(key, 6)
    for axis_at, parts in cuts:
        steps = jnp.exp(jax.random.uniform(jax.random.fold_in(own, axis_at), (parts,), jnp.float32, smallest / len(cuts), high / len(cuts)))
        factor_of = factor_of * jnp.repeat(steps, dims[axis_at] // parts).reshape([-1 if axis == axis_at else 1 for axis in range(len(dims))])
    return factor_of


def scatter_about(stream_key, extent, deviation, limit, shards=(), held_as=jnp.bfloat16):
    values = jax.random.normal(stream_key, extent, jnp.float32) * deviation
    if len(shards) > 0:
        values = block_levels(stream_key, extent, shards, -0.22, 0.18) * values
    return jnp.clip(values, min=-limit, max=limit).astype(held_as)


def setup_inputs(seed: int = 0) -> dict:
    key_of = jax.random.split(jax.random.key(seed), 7)
    queries = draw_queries(jax.random.fold_in(key_of[6], 71), 0)
    encoder_states = draw_encoder_states(jax.random.fold_in(key_of[6], 71), 0)
    norm_gain = jnp.clip(1.0 + 0.15 * jax.random.normal(key_of[2], (DE,), jnp.float32), 0.25, 1.75)
    kv_weight = scatter_about(key_of[3], (N_SECTION, DE, 2, KVH * HD), DE ** -0.5, 0.125, ((0, 2), (1, 8), (3, 2)))
    span_len = draw_span_len(jax.random.fold_in(key_of[6], 71), 0)
    span_owner = draw_span_owner(jax.random.fold_in(key_of[6], 71), 0)
    return dict(queries=queries, encoder_states=encoder_states, norm_gain=norm_gain, kv_weight=kv_weight, span_len=span_len, span_owner=span_owner)


def normalize(states, norm_gain):
    widened = states.astype(jnp.float32)
    factor = lax.rsqrt(lax.optimization_barrier(jnp.mean(widened * widened, axis=-1, keepdims=True)) + 1e-05)
    return (widened * factor * norm_gain).astype(jnp.bfloat16)

def reference(queries, encoder_states, norm_gain, kv_weight, span_len, span_owner):
    owners = span_owner[:, None] == jnp.arange(N_BLK, dtype=jnp.int32)[None, :]
    slot_load = lax.optimization_barrier(jnp.sum(jnp.where(owners, span_len[:, None], 0), axis=0)).astype(jnp.int32)
    slot_ids = jnp.arange(SLOTS, dtype=jnp.int32)
    alive = slot_ids % CAP < slot_load[slot_ids // CAP]
    normed = lax.optimization_barrier(normalize(encoder_states, norm_gain))
    group_count = HEADS // KVH

    def one_section(inputs):
        section_queries, section_weight = inputs
        projected = jnp.einsum('sd,dtk->stk', normed.astype(jnp.float32), section_weight.astype(jnp.float32))
        key_rows = lax.optimization_barrier(projected[:, 0].astype(jnp.bfloat16)).reshape(SLOTS, KVH, HD)
        value_rows = lax.optimization_barrier(projected[:, 1].astype(jnp.bfloat16)).reshape(SLOTS, KVH, HD)
        query_grid = section_queries.reshape(QTOK, KVH, group_count, HD)

        def one_group(grouped):
            group_queries, group_keys, group_values = grouped
            scores = jnp.einsum('qjd,rd->qjr', group_queries.astype(jnp.float32), group_keys.astype(jnp.float32)) * HD ** (-0.5)
            scores = jnp.where(alive[None, None, :], scores, -1e+30)
            peak = lax.optimization_barrier(jnp.max(scores, axis=-1, keepdims=True))
            weights = jnp.where(alive[None, None, :], jnp.exp(scores - peak), 0.0)
            denominator = lax.optimization_barrier(jnp.sum(weights, axis=-1, keepdims=True))
            rounded = lax.optimization_barrier(weights.astype(jnp.bfloat16))
            numerator = jnp.einsum('qjr,rd->qjd', rounded.astype(jnp.float32), group_values.astype(jnp.float32))
            return (numerator / denominator).astype(jnp.bfloat16)
        outputs = lax.map(one_group, (jnp.moveaxis(query_grid, 1, 0), jnp.moveaxis(key_rows, 1, 0), jnp.moveaxis(value_rows, 1, 0)))
        return jnp.moveaxis(outputs, 0, 1).reshape(QTOK, HEADS * HD)
    return lax.map(one_section, (queries, kv_weight))
```

```python
import functools

import jax
import jax.numpy as jnp
from jax import lax
from jax.experimental import pallas as pl
from jax.experimental.pallas import tpu as pltpu
from jax.sharding import PartitionSpec as P

HEADS = 32
KVH = 4
HD = 128
MEAN = 36
LOG2E = 1.4426950408889634

VMEM_SPEC = pl.BlockSpec(memory_space=pltpu.VMEM)


def normalize(states, norm_gain):
    widened = states.astype(jnp.float32)
    factor = lax.rsqrt(jnp.mean(widened * widened, axis=-1, keepdims=True) + 1e-05)
    return (widened * factor * norm_gain).astype(jnp.bfloat16)


def live_positions(span_len, span_owner, blocks, sections, cores, rows):
    shape = (sections, blocks, cores, rows)
    section, block, core, row = (lax.broadcasted_iota(jnp.int32, shape, axis).reshape(-1) for axis in range(4))
    within = (section * cores + core) * rows + row
    owner = span_owner[:, None]
    length = span_len[:, None]
    load = jnp.sum(jnp.where(owner == block[None, :], length, 0), axis=0)
    before = jnp.sum(jnp.where(owner < block[None, :], length, 0), axis=0)
    return jnp.where(within < load, before + within, -1)[None, :]


def project_kernel(position_ref, rows_ref, weight_ref, partial_ref):
    tiles = weight_ref.shape[1] // HD
    group_rows = partial_ref.shape[1]
    groups = partial_ref.shape[0] // tiles
    position = position_ref[...]
    rows = rows_ref[...]
    weight = weight_ref[...]
    for group in range(groups):
        wanted = lax.broadcasted_iota(jnp.int32, (group_rows, rows.shape[0]), 0) + group * group_rows
        pick = jnp.where(wanted == position, 1.0, 0.0).astype(jnp.bfloat16)
        picked = jnp.dot(pick, rows, preferred_element_type=jnp.float32).astype(jnp.bfloat16)
        projected = jnp.dot(picked, weight, preferred_element_type=jnp.float32).astype(jnp.bfloat16)
        for tile in range(tiles):
            partial_ref[tile * groups + group] = projected[:, tile * HD:(tile + 1) * HD]


def attend_kernel(query_ref, key_ref, value_ref, out_ref):
    heads = query_ref.shape[1] // HD
    keys = key_ref[0]
    values = value_ref[0]
    for head in range(heads):
        span = slice(head * HD, (head + 1) * HD)
        scores = lax.dot_general(
            query_ref[:, span], keys, (((1,), (1,)), ((), ())), preferred_element_type=jnp.float32
        )
        peak = jnp.max(scores, axis=-1, keepdims=True)
        weights = jnp.exp2((scores - peak) * (LOG2E * HD ** -0.5))
        denominator = jnp.sum(weights, axis=-1, keepdims=True)
        numerator = jnp.dot(weights.astype(jnp.bfloat16), values, preferred_element_type=jnp.float32)
        out_ref[:, span] = (numerator / denominator).astype(jnp.bfloat16)


def local(queries, encoder_states, norm_gain, kv_weight, span_len, span_owner):
    sections, blocks, cores = (lax.axis_size(name) for name in ("section", "blk", "mp"))
    rows, width = encoder_states.shape
    depth = width // blocks
    local_groups = kv_weight.shape[3] // HD
    tiles = 2 * local_groups
    groups = blocks // tiles
    group_rows = MEAN * tiles
    query_rows, query_width = queries.shape[1:]
    axes = ("section", "blk", "mp")

    normed = normalize(encoder_states, norm_gain)
    columns = normed.reshape(rows, blocks, depth).transpose(1, 0, 2)
    outgoing = jnp.broadcast_to(columns[None, :, None], (sections, blocks, cores, rows, depth))
    incoming = lax.all_to_all(outgoing.reshape(-1, rows, depth), axes, 0, 0, tiled=True)

    position = live_positions(span_len, span_owner, blocks, sections, cores, rows)
    weight = kv_weight[0].reshape(depth, -1)
    partial = pl.pallas_call(
        project_kernel,
        out_shape=jax.ShapeDtypeStruct((blocks, group_rows, HD), jnp.bfloat16),
        in_specs=[VMEM_SPEC] * 3,
        out_specs=VMEM_SPEC,
        name="project",
    )(position, incoming.reshape(-1, depth), weight)

    exchanged = lax.all_to_all(partial, "blk", 0, 0, tiled=True)
    summed = jnp.sum(exchanged.astype(jnp.float32), axis=0).astype(jnp.bfloat16)
    shared = lax.all_to_all(
        jnp.broadcast_to(summed[None], (blocks, group_rows, HD)), "blk", 0, 0, tiled=True
    )
    keys_values = shared.reshape(tiles, groups * group_rows, HD)
    slots = groups * group_rows
    group_width = query_width // local_groups
    attended = pl.pallas_call(
        attend_kernel,
        grid=(local_groups,),
        out_shape=jax.ShapeDtypeStruct((query_rows, query_width), jnp.bfloat16),
        in_specs=[
            pl.BlockSpec((query_rows, group_width), lambda g: (0, g)),
            pl.BlockSpec((1, slots, HD), lambda g: (g, 0, 0)),
            pl.BlockSpec((1, slots, HD), lambda g: (g + local_groups, 0, 0)),
        ],
        out_specs=pl.BlockSpec((query_rows, group_width), lambda g: (0, g)),
        name="attend",
    )(queries[0], keys_values, keys_values)
    return attended[None]


def solution(mesh):
    in_specs = (
        P("section", "blk", "mp"),
        P(("blk", "section", "mp"), None),
        P(),
        P("section", "blk", None, "mp"),
        P(),
        P(),
    )
    out_specs = P("section", "blk", "mp")
    return jax.shard_map(local, mesh=mesh, in_specs=in_specs, out_specs=out_specs, check_vma=False)
```

```python
import functools

import jax
import jax.numpy as jnp
from jax import lax
from jax.experimental import pallas as pl
from jax.experimental.pallas import tpu as pltpu
from jax.sharding import PartitionSpec as P

HEADS = 32
KVH = 4
HD = 128
MEAN = 36
LOG2E = 1.4426950408889634

VMEM_SPEC = pl.BlockSpec(memory_space=pltpu.VMEM)
GRANT = pltpu.CompilerParams(vmem_limit_bytes=16 << 20)


def normalize(states, norm_gain):
    widened = states.astype(jnp.float32)
    factor = lax.rsqrt(jnp.mean(widened * widened, axis=-1, keepdims=True) + 1e-05)
    return (widened * factor * norm_gain).astype(jnp.bfloat16)


def normalize_kernel(states_ref, gain_ref, out_ref):
    sections, blocks, cores, _, depth = out_ref.shape
    normed = normalize(states_ref[...], gain_ref[...])
    for block in range(blocks):
        columns = normed[:, block * depth:(block + 1) * depth]
        for section in range(sections):
            for core in range(cores):
                out_ref[section, block, core] = columns


def column_blocks(states, norm_gain, sections, blocks, cores):
    rows, width = states.shape
    depth = width // blocks
    shape = (sections, blocks, cores, rows, depth)
    if depth % HD == 0 and rows % 16 == 0:
        out = pl.pallas_call(
            normalize_kernel,
            out_shape=jax.ShapeDtypeStruct(shape, jnp.bfloat16),
            in_specs=[VMEM_SPEC] * 2,
            out_specs=VMEM_SPEC,
            compiler_params=GRANT,
            name="normalize",
        )(states, norm_gain[None, :])
    else:
        columns = normalize(states, norm_gain).reshape(rows, blocks, depth).transpose(1, 0, 2)
        out = jnp.broadcast_to(columns[None, :, None], shape)
    return out.reshape(-1, rows, depth)


def live_positions(span_len, span_owner, blocks, sections, cores, rows):
    shape = (sections, blocks, cores, rows)
    section, block, core, row = (lax.broadcasted_iota(jnp.int32, shape, axis).reshape(-1) for axis in range(4))
    within = (section * cores + core) * rows + row
    owner = span_owner[:, None]
    length = span_len[:, None]
    load = jnp.sum(jnp.where(owner == block[None, :], length, 0), axis=0)
    before = jnp.sum(jnp.where(owner < block[None, :], length, 0), axis=0)
    return jnp.where(within < load, before + within, -1)[None, :]


def project_kernel(position_ref, rows_ref, weight_ref, partial_ref):
    tiles = weight_ref.shape[1] // HD
    group_rows = partial_ref.shape[1]
    groups = partial_ref.shape[0] // tiles
    position = position_ref[...]
    rows = rows_ref[...]
    weight = weight_ref[...]
    step = 2 if groups % 2 == 0 else 1
    for first in range(0, groups, step):
        wanted = lax.broadcasted_iota(jnp.int32, (step * group_rows, rows.shape[0]), 0) + first * group_rows
        pick = jnp.where(wanted == position, 1.0, 0.0).astype(jnp.bfloat16)
        picked = jnp.dot(pick, rows, preferred_element_type=jnp.float32).astype(jnp.bfloat16)
        projected = jnp.dot(picked, weight, preferred_element_type=jnp.float32).astype(jnp.bfloat16)
        for group in range(step):
            for tile in range(tiles):
                partial_ref[tile * groups + first + group] = projected[
                    group * group_rows:(group + 1) * group_rows, tile * HD:(tile + 1) * HD
                ]


def sum_kernel(parts_ref, out_ref):
    total = parts_ref[0].astype(jnp.float32)
    for part in range(1, parts_ref.shape[0]):
        total += parts_ref[part].astype(jnp.float32)
    total = total.astype(jnp.bfloat16)
    for part in range(out_ref.shape[0]):
        out_ref[part] = total


def attend_kernel(query_ref, key_ref, value_ref, out_ref):
    heads = query_ref.shape[1] // HD
    count = query_ref.shape[0]
    stacked = jnp.concatenate([query_ref[:, head * HD:(head + 1) * HD] for head in range(heads)], axis=0)
    scores = lax.dot_general(
        stacked, key_ref[0], (((1,), (1,)), ((), ())), preferred_element_type=jnp.float32
    )
    peak = jnp.max(scores, axis=-1, keepdims=True)
    weights = jnp.exp2((scores - peak) * (LOG2E * HD ** -0.5))
    denominator = jnp.sum(weights, axis=-1, keepdims=True)
    numerator = jnp.dot(weights.astype(jnp.bfloat16), value_ref[0], preferred_element_type=jnp.float32)
    attended = (numerator * (1.0 / denominator)).astype(jnp.bfloat16)
    for head in range(heads):
        out_ref[:, head * HD:(head + 1) * HD] = attended[head * count:(head + 1) * count]


def local(queries, encoder_states, norm_gain, kv_weight, span_len, span_owner):
    sections, blocks, cores = (lax.axis_size(name) for name in ("section", "blk", "mp"))
    rows, width = encoder_states.shape
    depth = width // blocks
    local_groups = kv_weight.shape[3] // HD
    tiles = 2 * local_groups
    groups = blocks // tiles
    group_rows = MEAN * tiles
    query_rows, query_width = queries.shape[1:]
    axes = ("section", "blk", "mp")

    outgoing = column_blocks(encoder_states, norm_gain, sections, blocks, cores)
    incoming = lax.all_to_all(outgoing, axes, 0, 0, tiled=True)

    position = live_positions(span_len, span_owner, blocks, sections, cores, rows)
    weight = kv_weight[0].reshape(depth, -1)
    partial = pl.pallas_call(
        project_kernel,
        out_shape=jax.ShapeDtypeStruct((blocks, group_rows, HD), jnp.bfloat16),
        in_specs=[VMEM_SPEC] * 3,
        out_specs=VMEM_SPEC,
        compiler_params=GRANT,
        name="project",
    )(position, incoming.reshape(-1, depth), weight)

    exchanged = lax.all_to_all(partial, "blk", 0, 0, tiled=True)
    summed = pl.pallas_call(
        sum_kernel,
        out_shape=jax.ShapeDtypeStruct((blocks, group_rows, HD), jnp.bfloat16),
        in_specs=[VMEM_SPEC],
        out_specs=VMEM_SPEC,
        compiler_params=GRANT,
        name="sum",
    )(exchanged)
    shared = lax.all_to_all(summed, "blk", 0, 0, tiled=True)
    keys_values = shared.reshape(tiles, groups * group_rows, HD)
    slots = groups * group_rows
    group_width = query_width // local_groups
    attended = pl.pallas_call(
        attend_kernel,
        grid=(local_groups,),
        out_shape=jax.ShapeDtypeStruct((query_rows, query_width), jnp.bfloat16),
        in_specs=[
            pl.BlockSpec((query_rows, group_width), lambda g: (0, g)),
            pl.BlockSpec((1, slots, HD), lambda g: (g, 0, 0)),
            pl.BlockSpec((1, slots, HD), lambda g: (g + local_groups, 0, 0)),
        ],
        out_specs=pl.BlockSpec((query_rows, group_width), lambda g: (0, g)),
        compiler_params=GRANT,
        name="attend",
    )(queries[0], keys_values, keys_values)
    return attended[None]


def solution(mesh):
    in_specs = (
        P("section", "blk", "mp"),
        P(("blk", "section", "mp"), None),
        P(),
        P("section", "blk", None, "mp"),
        P(),
        P(),
    )
    out_specs = P("section", "blk", "mp")
    return jax.shard_map(local, mesh=mesh, in_specs=in_specs, out_specs=out_specs, check_vma=False)
```

```python
import jax
import jax.numpy as jnp
from jax import lax
from jax.experimental import pallas as pl
from jax.experimental.pallas import tpu as pltpu
from jax.sharding import PartitionSpec as P

HD = 128
MEAN = 36
LOG2E = 1.4426950408889634

VMEM_SPEC = pl.BlockSpec(memory_space=pltpu.VMEM)
GRANT = pltpu.CompilerParams(vmem_limit_bytes=16 << 20)


def normalize(states, norm_gain):
    widened = states.astype(jnp.float32)
    factor = lax.rsqrt(jnp.mean(widened * widened, axis=-1, keepdims=True) + 1e-05)
    return (widened * factor * norm_gain).astype(jnp.bfloat16)


def normalize_kernel(states_ref, gain_ref, out_ref):
    sections, blocks, _, width = out_ref.shape
    depth = width // 2
    normed = normalize(states_ref[...], gain_ref[...])
    for block in range(blocks):
        partner = (block + blocks // 2) % blocks
        for section in range(sections):
            out_ref[section, block, :, :depth] = normed[:, block * depth:(block + 1) * depth]
            out_ref[section, block, :, depth:] = normed[:, partner * depth:(partner + 1) * depth]


def column_blocks(states, norm_gain, sections, blocks):
    rows, width = states.shape
    depth = width // blocks
    shape = (sections, blocks, rows, 2 * depth)
    if depth % HD == 0 and rows % 16 == 0:
        out = pl.pallas_call(
            normalize_kernel,
            out_shape=jax.ShapeDtypeStruct(shape, jnp.bfloat16),
            in_specs=[VMEM_SPEC] * 2,
            out_specs=VMEM_SPEC,
            compiler_params=pltpu.CompilerParams(vmem_limit_bytes=60 << 20),
            name="normalize",
        )(states, norm_gain[None, :])
    else:
        columns = normalize(states, norm_gain).reshape(rows, blocks, depth).transpose(1, 0, 2)
        columns = jnp.concatenate([columns, jnp.roll(columns, -(blocks // 2), axis=0)], axis=2)
        out = jnp.broadcast_to(columns[None], shape)
    return out.reshape(-1, rows, 2 * depth)


def live_positions(span_len, span_owner, blocks, sections, cores, rows, core):
    index = lax.iota(jnp.int32, sections * blocks * rows)
    row = index % rows
    block = index // rows % blocks
    section = index // (rows * blocks)
    within = (section * cores + core) * rows + row
    owner = span_owner[:, None]
    length = span_len[:, None]
    load = jnp.sum(jnp.where(owner == block[None, :], length, 0), axis=0)
    before = jnp.sum(jnp.where(owner < block[None, :], length, 0), axis=0)
    return jnp.where(within < load, before + within, -1)[None, :]


def project_kernel(
    own_position_ref, other_position_ref, own_rows_ref, other_rows_ref, own_weight_ref, other_weight_ref, partial_ref
):
    depth, width = own_weight_ref.shape
    tiles = width // HD
    group_rows = partial_ref.shape[1]
    groups = partial_ref.shape[0] // tiles
    own_rows, other_rows = own_rows_ref[...], other_rows_ref[...]
    own_weight, other_weight = own_weight_ref[...], other_weight_ref[...]
    for group in range(groups):
        wanted = lax.broadcasted_iota(jnp.int32, (group_rows, own_rows.shape[0]), 0) + group * group_rows
        own_pick = jnp.where(wanted == own_position_ref[...], 1.0, 0.0).astype(jnp.bfloat16)
        other_pick = jnp.where(wanted == other_position_ref[...], 1.0, 0.0).astype(jnp.bfloat16)
        picked = jnp.dot(own_pick, own_rows, preferred_element_type=jnp.float32)
        picked += jnp.dot(other_pick, other_rows, preferred_element_type=jnp.float32)
        picked = picked.astype(jnp.bfloat16)
        projected = jnp.dot(picked[:, :depth], own_weight, preferred_element_type=jnp.float32)
        projected += jnp.dot(picked[:, depth:], other_weight, preferred_element_type=jnp.float32)
        projected = projected.astype(jnp.bfloat16)
        for tile in range(tiles):
            partial_ref[tile * groups + group] = projected[:, tile * HD:(tile + 1) * HD]


def sum_kernel(parts_ref, out_ref):
    total = parts_ref[0].astype(jnp.float32)
    for part in range(1, parts_ref.shape[0]):
        total += parts_ref[part].astype(jnp.float32)
    total = total.astype(jnp.bfloat16)
    for part in range(out_ref.shape[0]):
        out_ref[part] = total


def attend_kernel(query_ref, key_ref, value_ref, out_ref):
    heads = query_ref.shape[1] // HD
    count = query_ref.shape[0]
    stacked = jnp.concatenate([query_ref[:, head * HD:(head + 1) * HD] for head in range(heads)], axis=0)
    scores = lax.dot_general(
        stacked, key_ref[0], (((1,), (1,)), ((), ())), preferred_element_type=jnp.float32
    )
    peak = jnp.max(scores, axis=-1, keepdims=True)
    weights = jnp.exp2((scores - peak) * (LOG2E * HD ** -0.5))
    denominator = jnp.sum(weights, axis=-1, keepdims=True)
    numerator = jnp.dot(weights.astype(jnp.bfloat16), value_ref[0], preferred_element_type=jnp.float32)
    attended = (numerator * (1.0 / denominator)).astype(jnp.bfloat16)
    for head in range(heads):
        out_ref[:, head * HD:(head + 1) * HD] = attended[head * count:(head + 1) * count]


def local(queries, encoder_states, norm_gain, kv_weight, span_len, span_owner):
    sections, blocks, cores = (lax.axis_size(name) for name in ("section", "blk", "mp"))
    rows, width = encoder_states.shape
    depth = width // blocks
    local_groups = kv_weight.shape[3] // HD
    tiles = 2 * local_groups
    half = blocks // 2
    groups = half // tiles
    group_rows = MEAN * blocks // groups
    query_rows, query_width = queries.shape[1:]
    halves = [list(range(half)), list(range(half, blocks))]
    core = lax.axis_index("mp")

    other_weight = lax.ppermute(kv_weight, "blk", [(b, (b + half) % blocks) for b in range(blocks)])
    outgoing = column_blocks(encoder_states, norm_gain, sections, blocks)
    own_rows = lax.all_to_all(outgoing, ("section", "blk"), 0, 0, tiled=True)
    other_rows = lax.ppermute(own_rows, "mp", [(c, (c + 1) % cores) for c in range(cores)])

    own_position = live_positions(span_len, span_owner, blocks, sections, cores, rows, core)
    other_position = live_positions(span_len, span_owner, blocks, sections, cores, rows, cores - 1 - core)
    part_shape = jax.ShapeDtypeStruct((half, group_rows, HD), jnp.bfloat16)
    partial = pl.pallas_call(
        project_kernel,
        out_shape=part_shape,
        in_specs=[VMEM_SPEC] * 6,
        out_specs=VMEM_SPEC,
        compiler_params=GRANT,
        name="project",
    )(
        own_position,
        other_position,
        own_rows.reshape(-1, 2 * depth),
        other_rows.reshape(-1, 2 * depth),
        kv_weight[0].reshape(depth, -1),
        other_weight[0].reshape(depth, -1),
    )

    exchanged = lax.all_to_all(partial, "blk", 0, 0, tiled=True, axis_index_groups=halves)
    summed = pl.pallas_call(
        sum_kernel,
        out_shape=part_shape,
        in_specs=[VMEM_SPEC],
        out_specs=VMEM_SPEC,
        compiler_params=GRANT,
        name="sum",
    )(exchanged)
    shared = lax.all_to_all(summed, "blk", 0, 0, tiled=True, axis_index_groups=halves)
    keys_values = shared.reshape(tiles, groups * group_rows, HD)
    slots = groups * group_rows
    group_width = query_width // local_groups
    attended = pl.pallas_call(
        attend_kernel,
        grid=(local_groups,),
        out_shape=jax.ShapeDtypeStruct((query_rows, query_width), jnp.bfloat16),
        in_specs=[
            pl.BlockSpec((query_rows, group_width), lambda g: (0, g)),
            pl.BlockSpec((1, slots, HD), lambda g: (g, 0, 0)),
            pl.BlockSpec((1, slots, HD), lambda g: (g + local_groups, 0, 0)),
        ],
        out_specs=pl.BlockSpec((query_rows, group_width), lambda g: (0, g)),
        compiler_params=GRANT,
        name="attend",
    )(queries[0], keys_values, keys_values)
    return attended[None]


def solution(mesh):
    in_specs = (
        P("section", "blk", "mp"),
        P(("blk", "section", "mp"), None),
        P(),
        P("section", "blk", None, "mp"),
        P(),
        P(),
    )
    out_specs = P("section", "blk", "mp")
    return jax.shard_map(local, mesh=mesh, in_specs=in_specs, out_specs=out_specs, check_vma=False)
```

```python
import jax
import jax.numpy as jnp
from jax import lax
from jax.experimental import pallas as pl
from jax.experimental.pallas import tpu as pltpu
from jax.sharding import PartitionSpec as P

HD = 128
MEAN = 36
LOG2E = 1.4426950408889634

VMEM_SPEC = pl.BlockSpec(memory_space=pltpu.VMEM)
GRANT = pltpu.CompilerParams(vmem_limit_bytes=16 << 20)
WIDE_GRANT = pltpu.CompilerParams(vmem_limit_bytes=60 << 20)


def normalize(states, norm_gain):
    widened = states.astype(jnp.float32)
    factor = lax.rsqrt(jnp.mean(widened * widened, axis=-1, keepdims=True) + 1e-05)
    return (widened * factor * norm_gain).astype(jnp.bfloat16)


def normalize_kernel(states_ref, gain_ref, out_ref):
    sections, blocks, _, width = out_ref.shape
    depth = width // 2
    normed = normalize(states_ref[...], gain_ref[...])
    for block in range(blocks):
        partner = (block + blocks // 2) % blocks
        for section in range(sections):
            out_ref[section, block, :, :depth] = normed[:, block * depth:(block + 1) * depth]
            out_ref[section, block, :, depth:] = normed[:, partner * depth:(partner + 1) * depth]


def column_blocks(states, norm_gain, sections, blocks):
    rows, width = states.shape
    depth = width // blocks
    shape = (sections, blocks, rows, 2 * depth)
    if depth % HD == 0 and rows % 16 == 0:
        out = pl.pallas_call(
            normalize_kernel,
            out_shape=jax.ShapeDtypeStruct(shape, jnp.bfloat16),
            in_specs=[VMEM_SPEC] * 2,
            out_specs=VMEM_SPEC,
            compiler_params=WIDE_GRANT,
            name="normalize",
        )(states, norm_gain[None, :])
    else:
        columns = normalize(states, norm_gain).reshape(rows, blocks, depth).transpose(1, 0, 2)
        columns = jnp.concatenate([columns, jnp.roll(columns, -(blocks // 2), axis=0)], axis=2)
        out = jnp.broadcast_to(columns[None], shape)
    return out.reshape(-1, rows, 2 * depth)


def live_positions(span_len, span_owner, blocks, sections, cores, rows, core):
    index = lax.iota(jnp.int32, sections * blocks * rows)
    row = index % rows
    block = index // rows % blocks
    section = index // (rows * blocks)
    within = (section * cores + core) * rows + row
    owner = span_owner[:, None]
    length = span_len[:, None]
    load = jnp.sum(jnp.where(owner == block[None, :], length, 0), axis=0)
    before = jnp.sum(jnp.where(owner < block[None, :], length, 0), axis=0)
    return jnp.where(within < load, before + within, -1)[None, :]


def project_kernel(
    own_position_ref,
    other_position_ref,
    own_rows_ref,
    other_rows_ref,
    own_weight_ref,
    other_weight_ref,
    key_ref,
    value_ref,
    key_part_ref,
    value_part_ref,
):
    depth = own_weight_ref.shape[0]
    slots, width = key_ref.shape
    own_rows = own_rows_ref[...]
    wanted = lax.broadcasted_iota(jnp.int32, (slots, own_rows.shape[0]), 0)
    own_pick = jnp.where(wanted == own_position_ref[...], 1.0, 0.0).astype(jnp.bfloat16)
    other_pick = jnp.where(wanted == other_position_ref[...], 1.0, 0.0).astype(jnp.bfloat16)
    picked = jnp.dot(own_pick, own_rows, preferred_element_type=jnp.float32)
    picked += jnp.dot(other_pick, other_rows_ref[...], preferred_element_type=jnp.float32)
    picked = picked.astype(jnp.bfloat16)
    projected = jnp.dot(picked[:, :depth], own_weight_ref[...], preferred_element_type=jnp.float32)
    projected += jnp.dot(picked[:, depth:], other_weight_ref[...], preferred_element_type=jnp.float32)
    key_ref[...] = projected[:, :width]
    value_ref[...] = projected[:, width:]
    key_part_ref[...] = projected[:, :width].astype(jnp.bfloat16)
    value_part_ref[...] = projected[:, width:].astype(jnp.bfloat16)


def add_kernel(own_ref, received_ref, sum_ref, part_ref):
    total = own_ref[...] + received_ref[...].astype(jnp.float32)
    sum_ref[...] = total
    part_ref[...] = total.astype(jnp.bfloat16)


def add(own, received):
    return pl.pallas_call(
        add_kernel,
        out_shape=(
            jax.ShapeDtypeStruct(own.shape, jnp.float32),
            jax.ShapeDtypeStruct(own.shape, jnp.bfloat16),
        ),
        in_specs=[VMEM_SPEC] * 2,
        out_specs=(VMEM_SPEC,) * 2,
        compiler_params=GRANT,
        name="add",
    )(own, received)


def attend_kernel(query_ref, key_ref, key_part_ref, value_ref, value_part_ref, out_ref):
    heads = query_ref.shape[1] // HD
    count = query_ref.shape[0]
    keys = (key_ref[...] + key_part_ref[...].astype(jnp.float32)).astype(jnp.bfloat16)
    values = (value_ref[...] + value_part_ref[...].astype(jnp.float32)).astype(jnp.bfloat16)
    stacked = jnp.concatenate([query_ref[:, head * HD:(head + 1) * HD] for head in range(heads)], axis=0)
    scores = lax.dot_general(stacked, keys, (((1,), (1,)), ((), ())), preferred_element_type=jnp.float32)
    peak = jnp.max(scores, axis=-1, keepdims=True)
    weights = jnp.exp2((scores - peak) * (LOG2E * HD ** -0.5))
    denominator = jnp.sum(weights, axis=-1, keepdims=True)
    numerator = jnp.dot(weights.astype(jnp.bfloat16), values, preferred_element_type=jnp.float32)
    attended = (numerator * (1.0 / denominator)).astype(jnp.bfloat16)
    for head in range(heads):
        out_ref[:, head * HD:(head + 1) * HD] = attended[head * count:(head + 1) * count]


def local(queries, encoder_states, norm_gain, kv_weight, span_len, span_owner):
    sections, blocks, cores = (lax.axis_size(name) for name in ("section", "blk", "mp"))
    rows, features = encoder_states.shape
    depth = features // blocks
    local_groups = kv_weight.shape[3] // HD
    half = blocks // 2
    slots = MEAN * blocks
    query_rows, query_width = queries.shape[1:]
    core = lax.axis_index("mp")

    other_weight = lax.ppermute(kv_weight, "blk", [(b, (b + half) % blocks) for b in range(blocks)])
    outgoing = column_blocks(encoder_states, norm_gain, sections, blocks)
    own_rows = lax.all_to_all(outgoing, ("section", "blk"), 0, 0, tiled=True)
    other_rows = lax.ppermute(own_rows, "mp", [(c, (c + 1) % cores) for c in range(cores)])

    own_position = live_positions(span_len, span_owner, blocks, sections, cores, rows, core)
    other_position = live_positions(span_len, span_owner, blocks, sections, cores, rows, cores - 1 - core)
    width = kv_weight.shape[3]
    keys, values, key_part, value_part = pl.pallas_call(
        project_kernel,
        out_shape=(jax.ShapeDtypeStruct((slots, width), jnp.float32),) * 2
        + (jax.ShapeDtypeStruct((slots, width), jnp.bfloat16),) * 2,
        in_specs=[VMEM_SPEC] * 6,
        out_specs=(VMEM_SPEC,) * 4,
        compiler_params=GRANT,
        name="project",
    )(
        own_position,
        other_position,
        own_rows.reshape(-1, 2 * depth),
        other_rows.reshape(-1, 2 * depth),
        kv_weight[0].reshape(depth, -1),
        other_weight[0].reshape(depth, -1),
    )

    bits = [1 << place for place in range((half - 1).bit_length())]
    for step, (key_bit, value_bit) in enumerate(zip(bits, bits[1:] + bits[:1])):
        if step > 0:
            keys, key_part = add(keys, key_part)
            values, value_part = add(values, value_part)
        key_part = lax.ppermute(key_part, "blk", [(b, b ^ key_bit) for b in range(blocks)])
        value_part = lax.ppermute(value_part, "blk", [(b, b ^ value_bit) for b in range(blocks)])

    group_width = query_width // local_groups
    query_spec = pl.BlockSpec((query_rows, group_width), lambda g: (0, g))
    slot_spec = pl.BlockSpec((slots, HD), lambda g: (0, g))
    attended = pl.pallas_call(
        attend_kernel,
        grid=(local_groups,),
        out_shape=jax.ShapeDtypeStruct((query_rows, query_width), jnp.bfloat16),
        in_specs=[query_spec] + [slot_spec] * 4,
        out_specs=query_spec,
        compiler_params=GRANT,
        name="attend",
    )(queries[0], keys, key_part, values, value_part)
    return attended[None]


def solution(mesh):
    in_specs = (
        P("section", "blk", "mp"),
        P(("blk", "section", "mp"), None),
        P(),
        P("section", "blk", None, "mp"),
        P(),
        P(),
    )
    out_specs = P("section", "blk", "mp")
    return jax.shard_map(local, mesh=mesh, in_specs=in_specs, out_specs=out_specs, check_vma=False)
```

```python
import functools

import jax
import jax.numpy as jnp
from jax import lax
from jax.experimental import pallas as pl
from jax.experimental.pallas import tpu as pltpu
from jax.sharding import PartitionSpec as P

HD = 128
MEAN = 36
LOG2E = 1.4426950408889634

ANY_SPEC = pl.BlockSpec(memory_space=pl.ANY)
VMEM_SPEC = pl.BlockSpec(memory_space=pltpu.VMEM)
GRANT = pltpu.CompilerParams(vmem_limit_bytes=16 << 20)
WIDE_GRANT = pltpu.CompilerParams(vmem_limit_bytes=60 << 20)


def normalize(states, norm_gain):
    widened = states.astype(jnp.float32)
    factor = lax.rsqrt(jnp.mean(widened * widened, axis=-1, keepdims=True) + 1e-05)
    return (widened * factor * norm_gain).astype(jnp.bfloat16)


def normalize_kernel(states_ref, gain_ref, out_ref):
    sections, blocks, _, width = out_ref.shape
    depth = width // 2
    normed = normalize(states_ref[...], gain_ref[...])
    for block in range(blocks):
        partner = (block + blocks // 2) % blocks
        for section in range(sections):
            out_ref[section, block, :, :depth] = normed[:, block * depth:(block + 1) * depth]
            out_ref[section, block, :, depth:] = normed[:, partner * depth:(partner + 1) * depth]


def column_blocks(states, norm_gain, sections, blocks):
    rows, width = states.shape
    depth = width // blocks
    shape = (sections, blocks, rows, 2 * depth)
    if depth % HD == 0 and rows % 16 == 0:
        out = pl.pallas_call(
            normalize_kernel,
            out_shape=jax.ShapeDtypeStruct(shape, jnp.bfloat16),
            in_specs=[VMEM_SPEC] * 2,
            out_specs=VMEM_SPEC,
            compiler_params=WIDE_GRANT,
            name="normalize",
        )(states, norm_gain[None, :])
    else:
        columns = normalize(states, norm_gain).reshape(rows, blocks, depth).transpose(1, 0, 2)
        columns = jnp.concatenate([columns, jnp.roll(columns, -(blocks // 2), axis=0)], axis=2)
        out = jnp.broadcast_to(columns[None], shape)
    return out.reshape(-1, rows, 2 * depth)


def live_positions(span_len, span_owner, blocks, sections, cores, rows, core):
    index = lax.iota(jnp.int32, sections * blocks * rows)
    row = index % rows
    block = index // rows % blocks
    section = index // (rows * blocks)
    within = (section * cores + core) * rows + row
    owner = span_owner[:, None]
    length = span_len[:, None]
    load = jnp.sum(jnp.where(owner == block[None, :], length, 0), axis=0)
    before = jnp.sum(jnp.where(owner < block[None, :], length, 0), axis=0)
    return jnp.where(within < load, before + within, -1)[None, :]


def project_kernel(
    own_position_ref,
    other_position_ref,
    own_rows_ref,
    other_rows_ref,
    own_weight_ref,
    other_weight_ref,
    *out_refs,
):
    depth = own_weight_ref.shape[0]
    groups = len(out_refs) // 2
    slots = out_refs[0].shape[0]
    own_rows = own_rows_ref[...]
    wanted = lax.broadcasted_iota(jnp.int32, (slots, own_rows.shape[0]), 0)
    own_pick = jnp.where(wanted == own_position_ref[...], 1.0, 0.0).astype(jnp.bfloat16)
    other_pick = jnp.where(wanted == other_position_ref[...], 1.0, 0.0).astype(jnp.bfloat16)
    picked = jnp.dot(own_pick, own_rows, preferred_element_type=jnp.float32)
    picked += jnp.dot(other_pick, other_rows_ref[...], preferred_element_type=jnp.float32)
    picked = picked.astype(jnp.bfloat16)
    projected = jnp.dot(picked[:, :depth], own_weight_ref[...], preferred_element_type=jnp.float32)
    projected += jnp.dot(picked[:, depth:], other_weight_ref[...], preferred_element_type=jnp.float32)
    for group in range(groups):
        sum_ref, part_ref = out_refs[group], out_refs[groups + group]
        for kind in range(2):
            tile = kind * groups + group
            columns = projected[:, tile * HD:(tile + 1) * HD]
            sum_ref[:, kind * HD:(kind + 1) * HD] = columns
            part_ref[:, kind * HD:(kind + 1) * HD] = columns.astype(jnp.bfloat16)


def add_kernel(own_ref, received_ref, sum_ref, part_ref):
    total = own_ref[...] + received_ref[...].astype(jnp.float32)
    sum_ref[...] = total
    part_ref[...] = total.astype(jnp.bfloat16)


def add(own, received):
    return pl.pallas_call(
        add_kernel,
        out_shape=(
            jax.ShapeDtypeStruct(own.shape, jnp.float32),
            jax.ShapeDtypeStruct(own.shape, jnp.bfloat16),
        ),
        in_specs=[VMEM_SPEC] * 2,
        out_specs=(VMEM_SPEC,) * 2,
        compiler_params=GRANT,
        name="add",
    )(own, received)


def attend(group, heads, query_ref, sum_ref, part_ref, out_ref):
    count = query_ref.shape[0]
    first = group * heads
    total = (sum_ref[...] + part_ref[...].astype(jnp.float32)).astype(jnp.bfloat16)
    stacked = jnp.concatenate(
        [query_ref[:, head * HD:(head + 1) * HD] for head in range(first, first + heads)], axis=0
    )
    scores = lax.dot_general(stacked, total[:, :HD], (((1,), (1,)), ((), ())), preferred_element_type=jnp.float32)
    peak = jnp.max(scores, axis=-1, keepdims=True)
    weights = jnp.exp2((scores - peak) * (LOG2E * HD ** -0.5))
    denominator = jnp.sum(weights, axis=-1, keepdims=True)
    numerator = jnp.dot(weights.astype(jnp.bfloat16), total[:, HD:], preferred_element_type=jnp.float32)
    attended = (numerator * (1.0 / denominator)).astype(jnp.bfloat16)
    for head in range(heads):
        out_ref[:, head * HD:(head + 1) * HD] = attended[head * count:(head + 1) * count]


def attend_kernel(group, query_ref, sum_ref, part_ref, out_ref):
    attend(group, out_ref.shape[1] // HD, query_ref, sum_ref, part_ref, out_ref)


def last_attend_kernel(query_ref, sum_ref, part_ref, *rest):
    earlier, out_ref, stage, sem = rest[:-3], rest[-3], rest[-2], rest[-1]
    width = stage.shape[1]
    sources = (*earlier, stage)
    copies = [
        pltpu.make_async_copy(source, out_ref.at[:, group * width:(group + 1) * width], sem.at[group])
        for group, source in enumerate(sources)
    ]
    for copy in copies[:-1]:
        copy.start()
    attend(len(earlier), width // HD, query_ref, sum_ref, part_ref, stage)
    copies[-1].start()
    for copy in copies:
        copy.wait()


def local(queries, encoder_states, norm_gain, kv_weight, span_len, span_owner):
    sections, blocks, cores = (lax.axis_size(name) for name in ("section", "blk", "mp"))
    rows, features = encoder_states.shape
    depth = features // blocks
    local_groups = kv_weight.shape[3] // HD
    half = blocks // 2
    slots = MEAN * blocks
    query_rows, query_width = queries.shape[1:]
    core = lax.axis_index("mp")

    other_weight = lax.ppermute(kv_weight, "blk", [(b, (b + half) % blocks) for b in range(blocks)])
    outgoing = column_blocks(encoder_states, norm_gain, sections, blocks)
    own_rows = lax.all_to_all(outgoing, ("section", "blk"), 0, 0, tiled=True)
    other_rows = lax.ppermute(own_rows, "mp", [(c, (c + 1) % cores) for c in range(cores)])

    own_position = live_positions(span_len, span_owner, blocks, sections, cores, rows, core)
    other_position = live_positions(span_len, span_owner, blocks, sections, cores, rows, cores - 1 - core)
    outputs = pl.pallas_call(
        project_kernel,
        out_shape=(jax.ShapeDtypeStruct((slots, 2 * HD), jnp.float32),) * local_groups
        + (jax.ShapeDtypeStruct((slots, 2 * HD), jnp.bfloat16),) * local_groups,
        in_specs=[VMEM_SPEC] * 6,
        out_specs=(VMEM_SPEC,) * (2 * local_groups),
        compiler_params=GRANT,
        name="project",
    )(
        own_position,
        other_position,
        own_rows.reshape(-1, 2 * depth),
        other_rows.reshape(-1, 2 * depth),
        kv_weight[0].reshape(depth, -1),
        other_weight[0].reshape(depth, -1),
    )

    sums, parts = list(outputs[:local_groups]), list(outputs[local_groups:])
    bits = [1 << place for place in range((half - 1).bit_length())]
    for step in range(len(bits)):
        for group in range(local_groups):
            if step > 0:
                sums[group], parts[group] = add(sums[group], parts[group])
            bit = bits[(step + group) % len(bits)]
            parts[group] = lax.ppermute(parts[group], "blk", [(b, b ^ bit) for b in range(blocks)])

    group_shape = (query_rows, query_width // local_groups)
    attended = [
        pl.pallas_call(
            functools.partial(attend_kernel, group),
            out_shape=jax.ShapeDtypeStruct(group_shape, jnp.bfloat16),
            in_specs=[VMEM_SPEC] * 3,
            out_specs=VMEM_SPEC,
            compiler_params=GRANT,
            name="attend",
        )(queries[0], sums[group], parts[group])
        for group in range(local_groups - 1)
    ]
    attended = pl.pallas_call(
        last_attend_kernel,
        out_shape=jax.ShapeDtypeStruct((query_rows, query_width), jnp.bfloat16),
        in_specs=[VMEM_SPEC] * (2 + local_groups),
        out_specs=ANY_SPEC,
        scratch_shapes=[pltpu.VMEM(group_shape, jnp.bfloat16), pltpu.SemaphoreType.DMA((local_groups,))],
        compiler_params=GRANT,
        name="attend_last",
    )(queries[0], sums[-1], parts[-1], *attended)
    return attended[None]


def solution(mesh):
    in_specs = (
        P("section", "blk", "mp"),
        P(("blk", "section", "mp"), None),
        P(),
        P("section", "blk", None, "mp"),
        P(),
        P(),
    )
    out_specs = P("section", "blk", "mp")
    return jax.shard_map(local, mesh=mesh, in_specs=in_specs, out_specs=out_specs, check_vma=False)
```

```python
import functools

import jax
import jax.numpy as jnp
from jax import lax
from jax.experimental import pallas as pl
from jax.experimental.pallas import tpu as pltpu
from jax.sharding import PartitionSpec as P

HD = 128
MEAN = 36
LOG2E = 1.4426950408889634

ANY_SPEC = pl.BlockSpec(memory_space=pl.ANY)
VMEM_SPEC = pl.BlockSpec(memory_space=pltpu.VMEM)
GRANT = pltpu.CompilerParams(vmem_limit_bytes=16 << 20)
WIDE_GRANT = pltpu.CompilerParams(vmem_limit_bytes=60 << 20)


def normalize(states, norm_gain):
    widened = states.astype(jnp.float32)
    factor = lax.rsqrt(jnp.mean(widened * widened, axis=-1, keepdims=True) + 1e-05)
    return (widened * factor * norm_gain).astype(jnp.bfloat16)


def normalize_kernel(states_ref, gain_ref, out_ref):
    sections, blocks, _, width = out_ref.shape
    depth = width // 2
    normed = normalize(states_ref[...], gain_ref[...])
    for block in range(blocks):
        partner = (block + blocks // 2) % blocks
        for section in range(sections):
            out_ref[section, block, :, :depth] = normed[:, block * depth:(block + 1) * depth]
            out_ref[section, block, :, depth:] = normed[:, partner * depth:(partner + 1) * depth]


def column_blocks(states, norm_gain, sections, blocks):
    rows, width = states.shape
    depth = width // blocks
    shape = (sections, blocks, rows, 2 * depth)
    if depth % HD == 0 and rows % 16 == 0:
        out = pl.pallas_call(
            normalize_kernel,
            out_shape=jax.ShapeDtypeStruct(shape, jnp.bfloat16),
            in_specs=[VMEM_SPEC] * 2,
            out_specs=VMEM_SPEC,
            compiler_params=WIDE_GRANT,
            name="normalize",
        )(states, norm_gain[None, :])
    else:
        columns = normalize(states, norm_gain).reshape(rows, blocks, depth).transpose(1, 0, 2)
        columns = jnp.concatenate([columns, jnp.roll(columns, -(blocks // 2), axis=0)], axis=2)
        out = jnp.broadcast_to(columns[None], shape)
    return out.reshape(-1, rows, 2 * depth)


def live_positions(span_len, span_owner, blocks, sections, cores, rows, core):
    index = lax.iota(jnp.int32, sections * blocks * rows)
    row = index % rows
    block = index // rows % blocks
    section = index // (rows * blocks)
    within = (section * cores + core) * rows + row
    owner = span_owner[:, None]
    length = span_len[:, None]
    load = jnp.sum(jnp.where(owner == block[None, :], length, 0), axis=0)
    before = jnp.sum(jnp.where(owner < block[None, :], length, 0), axis=0)
    return jnp.where(within < load, before + within, -1)[None, :]


def project_kernel(
    own_position_ref,
    other_position_ref,
    own_rows_ref,
    other_rows_ref,
    own_weight_ref,
    other_weight_ref,
    *out_refs,
):
    depth = own_weight_ref.shape[0]
    groups = len(out_refs) // 2
    slots = out_refs[0].shape[0]
    own_rows = own_rows_ref[...]
    wanted = lax.broadcasted_iota(jnp.int32, (slots, own_rows.shape[0]), 0)
    own_pick = jnp.where(wanted == own_position_ref[...], 1.0, 0.0).astype(jnp.bfloat16)
    other_pick = jnp.where(wanted == other_position_ref[...], 1.0, 0.0).astype(jnp.bfloat16)
    picked = jnp.dot(own_pick, own_rows, preferred_element_type=jnp.float32)
    picked += jnp.dot(other_pick, other_rows_ref[...], preferred_element_type=jnp.float32)
    picked = picked.astype(jnp.bfloat16)
    projected = jnp.dot(picked[:, :depth], own_weight_ref[...], preferred_element_type=jnp.float32)
    projected += jnp.dot(picked[:, depth:], other_weight_ref[...], preferred_element_type=jnp.float32)
    for group in range(groups):
        sum_ref, part_ref = out_refs[group], out_refs[groups + group]
        for kind in range(2):
            tile = kind * groups + group
            sum_ref[:, kind * HD:(kind + 1) * HD] = projected[:, tile * HD:(tile + 1) * HD]
        pack(sum_ref[...], part_ref)


def pack(total, part_ref):
    keys = total[:, :HD]
    high = keys.astype(jnp.bfloat16)
    part_ref[:, :HD] = high
    part_ref[:, HD:2 * HD] = (keys - high.astype(jnp.float32)).astype(jnp.bfloat16)
    part_ref[:, 2 * HD:] = total[:, HD:].astype(jnp.bfloat16)


def summed(own_ref, received_ref):
    high, rest, values = (received_ref[:, k * HD:(k + 1) * HD].astype(jnp.float32) for k in range(3))
    return jnp.concatenate([own_ref[:, :HD] + (high + rest), own_ref[:, HD:] + values], axis=1)


def add_kernel(own_ref, received_ref, sum_ref, part_ref):
    total = summed(own_ref, received_ref)
    sum_ref[...] = total
    pack(total, part_ref)


def add(own, received):
    return pl.pallas_call(
        add_kernel,
        out_shape=(
            jax.ShapeDtypeStruct(own.shape, jnp.float32),
            jax.ShapeDtypeStruct(received.shape, jnp.bfloat16),
        ),
        in_specs=[VMEM_SPEC] * 2,
        out_specs=(VMEM_SPEC,) * 2,
        compiler_params=GRANT,
        name="add",
    )(own, received)


def attend(group, heads, query_ref, sum_ref, part_ref, out_ref):
    count = query_ref.shape[0]
    first = group * heads
    total = summed(sum_ref, part_ref).astype(jnp.bfloat16)
    stacked = jnp.concatenate(
        [query_ref[:, head * HD:(head + 1) * HD] for head in range(first, first + heads)], axis=0
    )
    scores = lax.dot_general(stacked, total[:, :HD], (((1,), (1,)), ((), ())), preferred_element_type=jnp.float32)
    peak = jnp.max(scores, axis=-1, keepdims=True)
    weights = jnp.exp2((scores - peak) * (LOG2E * HD ** -0.5))
    denominator = jnp.sum(weights, axis=-1, keepdims=True)
    numerator = jnp.dot(weights.astype(jnp.bfloat16), total[:, HD:], preferred_element_type=jnp.float32)
    attended = (numerator * (1.0 / denominator)).astype(jnp.bfloat16)
    for head in range(heads):
        out_ref[:, head * HD:(head + 1) * HD] = attended[head * count:(head + 1) * count]


def attend_kernel(group, query_ref, sum_ref, part_ref, out_ref):
    attend(group, out_ref.shape[1] // HD, query_ref, sum_ref, part_ref, out_ref)


def last_attend_kernel(query_ref, sum_ref, part_ref, *rest):
    earlier, out_ref, stage, sem = rest[:-3], rest[-3], rest[-2], rest[-1]
    width = stage.shape[1]
    sources = (*earlier, stage)
    copies = [
        pltpu.make_async_copy(source, out_ref.at[:, group * width:(group + 1) * width], sem.at[group])
        for group, source in enumerate(sources)
    ]
    for copy in copies[:-1]:
        copy.start()
    attend(len(earlier), width // HD, query_ref, sum_ref, part_ref, stage)
    copies[-1].start()
    for copy in copies:
        copy.wait()


def local(queries, encoder_states, norm_gain, kv_weight, span_len, span_owner):
    sections, blocks, cores = (lax.axis_size(name) for name in ("section", "blk", "mp"))
    rows, features = encoder_states.shape
    depth = features // blocks
    local_groups = kv_weight.shape[3] // HD
    half = blocks // 2
    slots = MEAN * blocks
    query_rows, query_width = queries.shape[1:]
    core = lax.axis_index("mp")

    other_weight = lax.ppermute(kv_weight, "blk", [(b, (b + half) % blocks) for b in range(blocks)])
    outgoing = column_blocks(encoder_states, norm_gain, sections, blocks)
    own_rows = lax.all_to_all(outgoing, ("section", "blk"), 0, 0, tiled=True)
    other_rows = lax.ppermute(own_rows, "mp", [(c, (c + 1) % cores) for c in range(cores)])

    own_position = live_positions(span_len, span_owner, blocks, sections, cores, rows, core)
    other_position = live_positions(span_len, span_owner, blocks, sections, cores, rows, cores - 1 - core)
    outputs = pl.pallas_call(
        project_kernel,
        out_shape=(jax.ShapeDtypeStruct((slots, 2 * HD), jnp.float32),) * local_groups
        + (jax.ShapeDtypeStruct((slots, 3 * HD), jnp.bfloat16),) * local_groups,
        in_specs=[VMEM_SPEC] * 6,
        out_specs=(VMEM_SPEC,) * (2 * local_groups),
        compiler_params=GRANT,
        name="project",
    )(
        own_position,
        other_position,
        own_rows.reshape(-1, 2 * depth),
        other_rows.reshape(-1, 2 * depth),
        kv_weight[0].reshape(depth, -1),
        other_weight[0].reshape(depth, -1),
    )

    sums, parts = list(outputs[:local_groups]), list(outputs[local_groups:])
    bits = [1 << place for place in range((half - 1).bit_length())]
    for step in range(len(bits)):
        for group in range(local_groups):
            if step > 0:
                sums[group], parts[group] = add(sums[group], parts[group])
            bit = bits[(step + group) % len(bits)]
            parts[group] = lax.ppermute(parts[group], "blk", [(b, b ^ bit) for b in range(blocks)])

    group_shape = (query_rows, query_width // local_groups)
    attended = [
        pl.pallas_call(
            functools.partial(attend_kernel, group),
            out_shape=jax.ShapeDtypeStruct(group_shape, jnp.bfloat16),
            in_specs=[VMEM_SPEC] * 3,
            out_specs=VMEM_SPEC,
            compiler_params=GRANT,
            name="attend",
        )(queries[0], sums[group], parts[group])
        for group in range(local_groups - 1)
    ]
    attended = pl.pallas_call(
        last_attend_kernel,
        out_shape=jax.ShapeDtypeStruct((query_rows, query_width), jnp.bfloat16),
        in_specs=[VMEM_SPEC] * (2 + local_groups),
        out_specs=ANY_SPEC,
        scratch_shapes=[pltpu.VMEM(group_shape, jnp.bfloat16), pltpu.SemaphoreType.DMA((local_groups,))],
        compiler_params=GRANT,
        name="attend_last",
    )(queries[0], sums[-1], parts[-1], *attended)
    return attended[None]


def solution(mesh):
    in_specs = (
        P("section", "blk", "mp"),
        P(("blk", "section", "mp"), None),
        P(),
        P("section", "blk", None, "mp"),
        P(),
        P(),
    )
    out_specs = P("section", "blk", "mp")
    return jax.shard_map(local, mesh=mesh, in_specs=in_specs, out_specs=out_specs, check_vma=False)
```

```python
import functools

import jax
import jax.numpy as jnp
from jax import lax
from jax.experimental import pallas as pl
from jax.experimental.pallas import tpu as pltpu
from jax.sharding import PartitionSpec as P

HD = 128
MEAN = 36
LOG2E = 1.4426950408889634

ANY_SPEC = pl.BlockSpec(memory_space=pl.ANY)
VMEM_SPEC = pl.BlockSpec(memory_space=pltpu.VMEM)
GRANT = pltpu.CompilerParams(vmem_limit_bytes=16 << 20)
WIDE_GRANT = pltpu.CompilerParams(vmem_limit_bytes=60 << 20)


def normalize(states, norm_gain):
    widened = states.astype(jnp.float32)
    factor = lax.rsqrt(jnp.mean(widened * widened, axis=-1, keepdims=True) + 1e-05)
    return (widened * factor * norm_gain).astype(jnp.bfloat16)


def normalize_kernel(states_ref, gain_ref, out_ref):
    sections, blocks, _, width = out_ref.shape
    depth = width // 2
    normed = normalize(states_ref[...], gain_ref[...])
    for block in range(blocks):
        partner = (block + blocks // 2) % blocks
        for section in range(sections):
            out_ref[section, block, :, :depth] = normed[:, block * depth:(block + 1) * depth]
            out_ref[section, block, :, depth:] = normed[:, partner * depth:(partner + 1) * depth]


def column_blocks(states, norm_gain, sections, blocks):
    rows, width = states.shape
    depth = width // blocks
    shape = (sections, blocks, rows, 2 * depth)
    if depth % HD == 0 and rows % 16 == 0:
        out = pl.pallas_call(
            normalize_kernel,
            out_shape=jax.ShapeDtypeStruct(shape, jnp.bfloat16),
            in_specs=[VMEM_SPEC] * 2,
            out_specs=VMEM_SPEC,
            compiler_params=WIDE_GRANT,
            name="normalize",
        )(states, norm_gain[None, :])
    else:
        columns = normalize(states, norm_gain).reshape(rows, blocks, depth).transpose(1, 0, 2)
        columns = jnp.concatenate([columns, jnp.roll(columns, -(blocks // 2), axis=0)], axis=2)
        out = jnp.broadcast_to(columns[None], shape)
    return out.reshape(-1, rows, 2 * depth)


def live_positions(span_len, span_owner, blocks, sections, cores, rows, core):
    index = lax.iota(jnp.int32, sections * blocks * rows)
    row = index % rows
    block = index // rows % blocks
    section = index // (rows * blocks)
    within = (section * cores + core) * rows + row
    owner = span_owner[:, None]
    length = span_len[:, None]
    load = jnp.sum(jnp.where(owner == block[None, :], length, 0), axis=0)
    before = jnp.sum(jnp.where(owner < block[None, :], length, 0), axis=0)
    return jnp.where(within < load, before + within, -1)[None, :]


def project_kernel(
    own_position_ref,
    other_position_ref,
    own_rows_ref,
    other_rows_ref,
    own_weight_ref,
    other_weight_ref,
    *out_refs,
):
    depth = own_weight_ref.shape[0]
    slots = out_refs[0].shape[0]
    own_rows = own_rows_ref[...]
    wanted = lax.broadcasted_iota(jnp.int32, (slots, own_rows.shape[0]), 0)
    own_pick = jnp.where(wanted == own_position_ref[...], 1.0, 0.0).astype(jnp.bfloat16)
    other_pick = jnp.where(wanted == other_position_ref[...], 1.0, 0.0).astype(jnp.bfloat16)
    picked = jnp.dot(own_pick, own_rows, preferred_element_type=jnp.float32)
    picked += jnp.dot(other_pick, other_rows_ref[...], preferred_element_type=jnp.float32)
    picked = picked.astype(jnp.bfloat16)
    projected = jnp.dot(picked[:, :depth], own_weight_ref[...], preferred_element_type=jnp.float32)
    projected += jnp.dot(picked[:, depth:], other_weight_ref[...], preferred_element_type=jnp.float32)
    chains = len(out_refs) // 2
    for chain in range(chains):
        total = projected[:, chain * HD:(chain + 1) * HD]
        out_refs[chain][...] = total
        pack(total, out_refs[chains + chain])


def pack(total, part_ref):
    high = total.astype(jnp.bfloat16)
    part_ref[:, :HD] = high
    if part_ref.shape[1] > HD:
        part_ref[:, HD:] = (total - high.astype(jnp.float32)).astype(jnp.bfloat16)


def summed(own_ref, received_ref):
    received = received_ref[:, :HD].astype(jnp.float32)
    if received_ref.shape[1] > HD:
        received += received_ref[:, HD:].astype(jnp.float32)
    return own_ref[...] + received


def add_kernel(own_ref, received_ref, sum_ref, part_ref):
    total = summed(own_ref, received_ref)
    sum_ref[...] = total
    pack(total, part_ref)


def add(own, received):
    return pl.pallas_call(
        add_kernel,
        out_shape=(
            jax.ShapeDtypeStruct(own.shape, jnp.float32),
            jax.ShapeDtypeStruct(received.shape, jnp.bfloat16),
        ),
        in_specs=[VMEM_SPEC] * 2,
        out_specs=(VMEM_SPEC,) * 2,
        compiler_params=GRANT,
        name="add",
    )(own, received)


def attend(group, heads, query_ref, key_ref, key_part_ref, value_ref, value_part_ref, out_ref):
    count = query_ref.shape[0]
    first = group * heads
    keys = summed(key_ref, key_part_ref).astype(jnp.bfloat16)
    values = summed(value_ref, value_part_ref).astype(jnp.bfloat16)
    stacked = jnp.concatenate(
        [query_ref[:, head * HD:(head + 1) * HD] for head in range(first, first + heads)], axis=0
    )
    scores = lax.dot_general(stacked, keys, (((1,), (1,)), ((), ())), preferred_element_type=jnp.float32)
    peak = jnp.max(scores, axis=-1, keepdims=True)
    weights = jnp.exp2((scores - peak) * (LOG2E * HD ** -0.5))
    denominator = jnp.sum(weights, axis=-1, keepdims=True)
    numerator = jnp.dot(weights.astype(jnp.bfloat16), values, preferred_element_type=jnp.float32)
    attended = (numerator * (1.0 / denominator)).astype(jnp.bfloat16)
    for head in range(heads):
        out_ref[:, head * HD:(head + 1) * HD] = attended[head * count:(head + 1) * count]


def attend_kernel(group, query_ref, *refs):
    attend(group, refs[-1].shape[1] // HD, query_ref, *refs)


def last_attend_kernel(query_ref, key_ref, key_part_ref, value_ref, value_part_ref, *rest):
    earlier, out_ref, stage, sem = rest[:-3], rest[-3], rest[-2], rest[-1]
    width = stage.shape[1]
    sources = (*earlier, stage)
    copies = [
        pltpu.make_async_copy(source, out_ref.at[:, group * width:(group + 1) * width], sem.at[group])
        for group, source in enumerate(sources)
    ]
    for copy in copies[:-1]:
        copy.start()
    attend(len(earlier), width // HD, query_ref, key_ref, key_part_ref, value_ref, value_part_ref, stage)
    copies[-1].start()
    for copy in copies:
        copy.wait()


def local(queries, encoder_states, norm_gain, kv_weight, span_len, span_owner):
    sections, blocks, cores = (lax.axis_size(name) for name in ("section", "blk", "mp"))
    rows, features = encoder_states.shape
    depth = features // blocks
    local_groups = kv_weight.shape[3] // HD
    half = blocks // 2
    slots = MEAN * blocks
    query_rows, query_width = queries.shape[1:]
    core = lax.axis_index("mp")

    other_weight = lax.ppermute(kv_weight, "blk", [(b, (b + half) % blocks) for b in range(blocks)])
    outgoing = column_blocks(encoder_states, norm_gain, sections, blocks)
    own_rows = lax.all_to_all(outgoing, ("section", "blk"), 0, 0, tiled=True)
    other_rows = lax.ppermute(own_rows, "mp", [(c, (c + 1) % cores) for c in range(cores)])

    own_position = live_positions(span_len, span_owner, blocks, sections, cores, rows, core)
    other_position = live_positions(span_len, span_owner, blocks, sections, cores, rows, cores - 1 - core)
    outputs = pl.pallas_call(
        project_kernel,
        out_shape=(jax.ShapeDtypeStruct((slots, HD), jnp.float32),) * (2 * local_groups)
        + (jax.ShapeDtypeStruct((slots, 2 * HD), jnp.bfloat16),) * local_groups
        + (jax.ShapeDtypeStruct((slots, HD), jnp.bfloat16),) * local_groups,
        in_specs=[VMEM_SPEC] * 6,
        out_specs=(VMEM_SPEC,) * (4 * local_groups),
        compiler_params=GRANT,
        name="project",
    )(
        own_position,
        other_position,
        own_rows.reshape(-1, 2 * depth),
        other_rows.reshape(-1, 2 * depth),
        kv_weight[0].reshape(depth, -1),
        other_weight[0].reshape(depth, -1),
    )

    chains = 2 * local_groups
    sums, parts = list(outputs[:chains]), list(outputs[chains:])
    bits = [1 << place for place in range((half - 1).bit_length())]
    for step in range(len(bits)):
        for chain in range(chains):
            if step > 0:
                sums[chain], parts[chain] = add(sums[chain], parts[chain])
            bit = bits[(step + chain) % len(bits)]
            parts[chain] = lax.ppermute(parts[chain], "blk", [(b, b ^ bit) for b in range(blocks)])

    def summands(group):
        return [refs[chain] for chain in (group, local_groups + group) for refs in (sums, parts)]

    group_shape = (query_rows, query_width // local_groups)
    attended = [
        pl.pallas_call(
            functools.partial(attend_kernel, group),
            out_shape=jax.ShapeDtypeStruct(group_shape, jnp.bfloat16),
            in_specs=[VMEM_SPEC] * 5,
            out_specs=VMEM_SPEC,
            compiler_params=GRANT,
            name="attend",
        )(queries[0], *summands(group))
        for group in range(local_groups - 1)
    ]
    attended = pl.pallas_call(
        last_attend_kernel,
        out_shape=jax.ShapeDtypeStruct((query_rows, query_width), jnp.bfloat16),
        in_specs=[VMEM_SPEC] * (4 + local_groups),
        out_specs=ANY_SPEC,
        scratch_shapes=[pltpu.VMEM(group_shape, jnp.bfloat16), pltpu.SemaphoreType.DMA((local_groups,))],
        compiler_params=GRANT,
        name="attend_last",
    )(queries[0], *summands(local_groups - 1), *attended)
    return attended[None]


def solution(mesh):
    in_specs = (
        P("section", "blk", "mp"),
        P(("blk", "section", "mp"), None),
        P(),
        P("section", "blk", None, "mp"),
        P(),
        P(),
    )
    out_specs = P("section", "blk", "mp")
    return jax.shard_map(local, mesh=mesh, in_specs=in_specs, out_specs=out_specs, check_vma=False)
```

```python
import functools

import jax
import jax.numpy as jnp
from jax import lax
from jax.experimental import pallas as pl
from jax.experimental.pallas import tpu as pltpu
from jax.sharding import PartitionSpec as P

HD = 128
MEAN = 36
LOG2E = 1.4426950408889634

ANY_SPEC = pl.BlockSpec(memory_space=pl.ANY)
VMEM_SPEC = pl.BlockSpec(memory_space=pltpu.VMEM)
GRANT = pltpu.CompilerParams(vmem_limit_bytes=16 << 20)
WIDE_GRANT = pltpu.CompilerParams(vmem_limit_bytes=60 << 20)


def normalize(states, norm_gain):
    widened = states.astype(jnp.float32)
    factor = lax.rsqrt(jnp.mean(widened * widened, axis=-1, keepdims=True) + 1e-05)
    return (widened * factor * norm_gain).astype(jnp.bfloat16)


def normalize_kernel(states_ref, gain_ref, out_ref):
    sections, blocks, _, width = out_ref.shape
    depth = width // 2
    normed = normalize(states_ref[...], gain_ref[...])
    for block in range(blocks):
        partner = (block + blocks // 2) % blocks
        for section in range(sections):
            out_ref[section, block, :, :depth] = normed[:, block * depth:(block + 1) * depth]
            out_ref[section, block, :, depth:] = normed[:, partner * depth:(partner + 1) * depth]


def column_blocks(states, norm_gain, sections, blocks):
    rows, width = states.shape
    depth = width // blocks
    shape = (sections, blocks, rows, 2 * depth)
    if depth % HD == 0 and rows % 16 == 0:
        out = pl.pallas_call(
            normalize_kernel,
            out_shape=jax.ShapeDtypeStruct(shape, jnp.bfloat16),
            in_specs=[VMEM_SPEC] * 2,
            out_specs=VMEM_SPEC,
            compiler_params=WIDE_GRANT,
            name="normalize",
        )(states, norm_gain[None, :])
    else:
        columns = normalize(states, norm_gain).reshape(rows, blocks, depth).transpose(1, 0, 2)
        columns = jnp.concatenate([columns, jnp.roll(columns, -(blocks // 2), axis=0)], axis=2)
        out = jnp.broadcast_to(columns[None], shape)
    return out.reshape(-1, rows, 2 * depth)


def live_positions(span_len, span_owner, blocks, sections, cores, rows, core):
    index = lax.iota(jnp.int32, sections * blocks * rows)
    row = index % rows
    block = index // rows % blocks
    section = index // (rows * blocks)
    within = (section * cores + core) * rows + row
    owner = span_owner[:, None]
    length = span_len[:, None]
    load = jnp.sum(jnp.where(owner == block[None, :], length, 0), axis=0)
    before = jnp.sum(jnp.where(owner < block[None, :], length, 0), axis=0)
    return jnp.where(within < load, before + within, -1)[None, :]


def project(picked, own_weight_ref, other_weight_ref, out_refs):
    depth = own_weight_ref.shape[0]
    chains = len(out_refs) // 2
    projected = jnp.dot(picked[:, :depth], own_weight_ref[...], preferred_element_type=jnp.float32)
    projected += jnp.dot(picked[:, depth:], other_weight_ref[...], preferred_element_type=jnp.float32)
    for chain in range(chains):
        total = projected[:, chain * HD:(chain + 1) * HD]
        out_refs[chain][...] = total
        pack(total, out_refs[chains + chain])


def key_kernel(
    own_position_ref,
    other_position_ref,
    own_rows_ref,
    other_rows_ref,
    own_weight_ref,
    other_weight_ref,
    picked_ref,
    *out_refs,
):
    own_rows = own_rows_ref[...]
    width = own_weight_ref.shape[1] // 2
    wanted = lax.broadcasted_iota(jnp.int32, (picked_ref.shape[0], own_rows.shape[0]), 0)
    own_pick = jnp.where(wanted == own_position_ref[...], 1.0, 0.0).astype(jnp.bfloat16)
    other_pick = jnp.where(wanted == other_position_ref[...], 1.0, 0.0).astype(jnp.bfloat16)
    picked = jnp.dot(own_pick, own_rows, preferred_element_type=jnp.float32)
    picked += jnp.dot(other_pick, other_rows_ref[...], preferred_element_type=jnp.float32)
    picked = picked.astype(jnp.bfloat16)
    picked_ref[...] = picked
    project(picked, own_weight_ref.at[:, :width], other_weight_ref.at[:, :width], out_refs)


def value_kernel(picked_ref, own_weight_ref, other_weight_ref, *out_refs):
    width = own_weight_ref.shape[1] // 2
    project(picked_ref[...], own_weight_ref.at[:, width:], other_weight_ref.at[:, width:], out_refs)


def pack(total, part_ref):
    high = total.astype(jnp.bfloat16)
    part_ref[:, :HD] = high
    if part_ref.shape[1] > HD:
        part_ref[:, HD:] = (total - high.astype(jnp.float32)).astype(jnp.bfloat16)


def summed(own_ref, received_ref):
    received = received_ref[:, :HD].astype(jnp.float32)
    if received_ref.shape[1] > HD:
        received += received_ref[:, HD:].astype(jnp.float32)
    return own_ref[...] + received


def add_kernel(own_ref, received_ref, sum_ref, part_ref):
    total = summed(own_ref, received_ref)
    sum_ref[...] = total
    pack(total, part_ref)


def add(own, received):
    return pl.pallas_call(
        add_kernel,
        out_shape=(
            jax.ShapeDtypeStruct(own.shape, jnp.float32),
            jax.ShapeDtypeStruct(received.shape, jnp.bfloat16),
        ),
        in_specs=[VMEM_SPEC] * 2,
        out_specs=(VMEM_SPEC,) * 2,
        compiler_params=GRANT,
        name="add",
    )(own, received)


def score_kernel(group, query_ref, key_ref, key_part_ref, weight_ref, inverse_ref):
    count = query_ref.shape[0]
    heads = weight_ref.shape[0] // count
    keys = summed(key_ref, key_part_ref).astype(jnp.bfloat16)
    stacked = jnp.concatenate(
        [query_ref[:, head * HD:(head + 1) * HD] for head in range(group * heads, (group + 1) * heads)], axis=0
    )
    scores = lax.dot_general(stacked, keys, (((1,), (1,)), ((), ())), preferred_element_type=jnp.float32)
    peak = jnp.max(scores, axis=-1, keepdims=True)
    weights = jnp.exp2((scores - peak) * (LOG2E * HD ** -0.5))
    weight_ref[...] = weights.astype(jnp.bfloat16)
    inverse_ref[...] = 1.0 / jnp.sum(weights, axis=-1, keepdims=True)


def mix(weight_ref, inverse_ref, value_ref, value_part_ref, out_ref):
    count = out_ref.shape[0]
    values = summed(value_ref, value_part_ref).astype(jnp.bfloat16)
    numerator = jnp.dot(weight_ref[...], values, preferred_element_type=jnp.float32)
    attended = (numerator * inverse_ref[...]).astype(jnp.bfloat16)
    for head in range(out_ref.shape[1] // HD):
        out_ref[:, head * HD:(head + 1) * HD] = attended[head * count:(head + 1) * count]


def last_mix_kernel(weight_ref, inverse_ref, value_ref, value_part_ref, *rest):
    earlier, out_ref, stage, sem = rest[:-3], rest[-3], rest[-2], rest[-1]
    width = stage.shape[1]
    sources = (*earlier, stage)
    copies = [
        pltpu.make_async_copy(source, out_ref.at[:, group * width:(group + 1) * width], sem.at[group])
        for group, source in enumerate(sources)
    ]
    for copy in copies[:-1]:
        copy.start()
    mix(weight_ref, inverse_ref, value_ref, value_part_ref, stage)
    copies[-1].start()
    for copy in copies:
        copy.wait()


def local(queries, encoder_states, norm_gain, kv_weight, span_len, span_owner):
    sections, blocks, cores = (lax.axis_size(name) for name in ("section", "blk", "mp"))
    rows, features = encoder_states.shape
    depth = features // blocks
    local_groups = kv_weight.shape[3] // HD
    half = blocks // 2
    slots = MEAN * blocks
    query_rows, query_width = queries.shape[1:]
    core = lax.axis_index("mp")

    other_weight = lax.ppermute(kv_weight, "blk", [(b, (b + half) % blocks) for b in range(blocks)])
    outgoing = column_blocks(encoder_states, norm_gain, sections, blocks)
    own_rows = lax.all_to_all(outgoing, ("section", "blk"), 0, 0, tiled=True)
    other_rows = lax.ppermute(own_rows, "mp", [(c, (c + 1) % cores) for c in range(cores)])

    own_position = live_positions(span_len, span_owner, blocks, sections, cores, rows, core)
    other_position = live_positions(span_len, span_owner, blocks, sections, cores, rows, cores - 1 - core)
    own_weight, other_weight = kv_weight[0].reshape(depth, -1), other_weight[0].reshape(depth, -1)
    sum_shapes = (jax.ShapeDtypeStruct((slots, HD), jnp.float32),) * local_groups
    picked, *key_outputs = pl.pallas_call(
        key_kernel,
        out_shape=(jax.ShapeDtypeStruct((slots, 2 * depth), jnp.bfloat16), *sum_shapes)
        + (jax.ShapeDtypeStruct((slots, 2 * HD), jnp.bfloat16),) * local_groups,
        in_specs=[VMEM_SPEC] * 6,
        out_specs=(VMEM_SPEC,) * (2 * local_groups + 1),
        compiler_params=GRANT,
        name="project_keys",
    )(
        own_position,
        other_position,
        own_rows.reshape(-1, 2 * depth),
        other_rows.reshape(-1, 2 * depth),
        own_weight,
        other_weight,
    )
    value_outputs = pl.pallas_call(
        value_kernel,
        out_shape=sum_shapes + (jax.ShapeDtypeStruct((slots, HD), jnp.bfloat16),) * local_groups,
        in_specs=[VMEM_SPEC] * 3,
        out_specs=(VMEM_SPEC,) * (2 * local_groups),
        compiler_params=GRANT,
        name="project_values",
    )(picked, own_weight, other_weight)

    chains = 2 * local_groups
    sums = [*key_outputs[:local_groups], *value_outputs[:local_groups]]
    parts = [*key_outputs[local_groups:], *value_outputs[local_groups:]]
    bits = [1 << place for place in range((half - 1).bit_length())]
    for step in range(len(bits)):
        for chain in range(chains):
            if step > 0:
                sums[chain], parts[chain] = add(sums[chain], parts[chain])
            bit = bits[(step + chain) % len(bits)]
            parts[chain] = lax.ppermute(parts[chain], "blk", [(b, b ^ bit) for b in range(blocks)])

    group_shape = (query_rows, query_width // local_groups)
    group_heads = query_width // local_groups // HD
    scored = [
        pl.pallas_call(
            functools.partial(score_kernel, group),
            out_shape=(
                jax.ShapeDtypeStruct((group_heads * query_rows, slots), jnp.bfloat16),
                jax.ShapeDtypeStruct((group_heads * query_rows, 1), jnp.float32),
            ),
            in_specs=[VMEM_SPEC] * 3,
            out_specs=(VMEM_SPEC,) * 2,
            compiler_params=GRANT,
            name="score",
        )(queries[0], sums[group], parts[group])
        for group in range(local_groups)
    ]
    operands = [(*scored[group], sums[local_groups + group], parts[local_groups + group]) for group in range(local_groups)]
    attended = [
        pl.pallas_call(
            mix,
            out_shape=jax.ShapeDtypeStruct(group_shape, jnp.bfloat16),
            in_specs=[VMEM_SPEC] * 4,
            out_specs=VMEM_SPEC,
            compiler_params=GRANT,
            name="mix",
        )(*operands[group])
        for group in range(local_groups - 1)
    ]
    attended = pl.pallas_call(
        last_mix_kernel,
        out_shape=jax.ShapeDtypeStruct((query_rows, query_width), jnp.bfloat16),
        in_specs=[VMEM_SPEC] * (3 + local_groups),
        out_specs=ANY_SPEC,
        scratch_shapes=[pltpu.VMEM(group_shape, jnp.bfloat16), pltpu.SemaphoreType.DMA((local_groups,))],
        compiler_params=GRANT,
        name="mix_last",
    )(*operands[-1], *attended)
    return attended[None]


def solution(mesh):
    in_specs = (
        P("section", "blk", "mp"),
        P(("blk", "section", "mp"), None),
        P(),
        P("section", "blk", None, "mp"),
        P(),
        P(),
    )
    out_specs = P("section", "blk", "mp")
    return jax.shard_map(local, mesh=mesh, in_specs=in_specs, out_specs=out_specs, check_vma=False)
```

```python
import functools

import jax
import jax.numpy as jnp
from jax import lax
from jax.experimental import pallas as pl
from jax.experimental.pallas import tpu as pltpu
from jax.sharding import PartitionSpec as P

HD = 128
MEAN = 36
LOG2E = 1.4426950408889634

ANY_SPEC = pl.BlockSpec(memory_space=pl.ANY)
VMEM_SPEC = pl.BlockSpec(memory_space=pltpu.VMEM)
GRANT = pltpu.CompilerParams(vmem_limit_bytes=16 << 20)
WIDE_GRANT = pltpu.CompilerParams(vmem_limit_bytes=60 << 20)


def normalize(states, norm_gain):
    widened = states.astype(jnp.float32)
    factor = lax.rsqrt(jnp.mean(widened * widened, axis=-1, keepdims=True) + 1e-05)
    return (widened * factor * norm_gain).astype(jnp.bfloat16)


def normalize_kernel(states_ref, gain_ref, out_ref):
    sections, blocks, _, width = out_ref.shape
    depth = width // 2
    normed = normalize(states_ref[...], gain_ref[...])
    for block in range(blocks):
        partner = (block + blocks // 2) % blocks
        for section in range(sections):
            out_ref[section, block, :, :depth] = normed[:, block * depth:(block + 1) * depth]
            out_ref[section, block, :, depth:] = normed[:, partner * depth:(partner + 1) * depth]


def column_blocks(states, norm_gain, sections, blocks):
    rows, width = states.shape
    depth = width // blocks
    shape = (sections, blocks, rows, 2 * depth)
    if depth % HD == 0 and rows % 16 == 0:
        out = pl.pallas_call(
            normalize_kernel,
            out_shape=jax.ShapeDtypeStruct(shape, jnp.bfloat16),
            in_specs=[VMEM_SPEC] * 2,
            out_specs=VMEM_SPEC,
            compiler_params=WIDE_GRANT,
            name="normalize",
        )(states, norm_gain[None, :])
    else:
        columns = normalize(states, norm_gain).reshape(rows, blocks, depth).transpose(1, 0, 2)
        columns = jnp.concatenate([columns, jnp.roll(columns, -(blocks // 2), axis=0)], axis=2)
        out = jnp.broadcast_to(columns[None], shape)
    return out.reshape(-1, rows, 2 * depth)


def live_positions(span_len, span_owner, blocks, sections, cores, rows, core):
    index = lax.iota(jnp.int32, sections * blocks * rows)
    row = index % rows
    block = index // rows % blocks
    section = index // (rows * blocks)
    within = (section * cores + core) * rows + row
    owner = span_owner[:, None]
    length = span_len[:, None]
    load = jnp.sum(jnp.where(owner == block[None, :], length, 0), axis=0)
    before = jnp.sum(jnp.where(owner < block[None, :], length, 0), axis=0)
    return jnp.where(within < load, before + within, -1)[None, :]


def project_kernel(
    own_position_ref,
    other_position_ref,
    own_rows_ref,
    other_rows_ref,
    own_weight_ref,
    other_weight_ref,
    *out_refs,
):
    depth = own_weight_ref.shape[0]
    slots = out_refs[0].shape[0]
    own_rows = own_rows_ref[...]
    wanted = lax.broadcasted_iota(jnp.int32, (slots, own_rows.shape[0]), 0)
    own_pick = jnp.where(wanted == own_position_ref[...], 1.0, 0.0).astype(jnp.bfloat16)
    other_pick = jnp.where(wanted == other_position_ref[...], 1.0, 0.0).astype(jnp.bfloat16)
    picked = jnp.dot(own_pick, own_rows, preferred_element_type=jnp.float32)
    picked += jnp.dot(other_pick, other_rows_ref[...], preferred_element_type=jnp.float32)
    picked = picked.astype(jnp.bfloat16)
    projected = jnp.dot(picked[:, :depth], own_weight_ref[...], preferred_element_type=jnp.float32)
    projected += jnp.dot(picked[:, depth:], other_weight_ref[...], preferred_element_type=jnp.float32)
    chains = len(out_refs) // 2
    for chain in range(chains):
        total = projected[:, chain * HD:(chain + 1) * HD]
        out_refs[chain][...] = total
        pack(total, out_refs[chains + chain])


def pack(total, part_ref):
    high = total.astype(jnp.bfloat16)
    part_ref[:, :HD] = high
    if part_ref.shape[1] > HD:
        part_ref[:, HD:] = (total - high.astype(jnp.float32)).astype(jnp.bfloat16)


def summed(own_ref, received_ref):
    received = received_ref[:, :HD].astype(jnp.float32)
    if received_ref.shape[1] > HD:
        received += received_ref[:, HD:].astype(jnp.float32)
    return own_ref[...] + received


def add_kernel(own_ref, received_ref, sum_ref, part_ref):
    total = summed(own_ref, received_ref)
    sum_ref[...] = total
    pack(total, part_ref)


def add(own, received):
    return pl.pallas_call(
        add_kernel,
        out_shape=(
            jax.ShapeDtypeStruct(own.shape, jnp.float32),
            jax.ShapeDtypeStruct(received.shape, jnp.bfloat16),
        ),
        in_specs=[VMEM_SPEC] * 2,
        out_specs=(VMEM_SPEC,) * 2,
        compiler_params=GRANT,
        name="add",
    )(own, received)


def score_kernel(group, query_ref, key_ref, key_part_ref, weight_ref, inverse_ref):
    count = query_ref.shape[0]
    heads = weight_ref.shape[0] // count
    keys = summed(key_ref, key_part_ref).astype(jnp.bfloat16)
    stacked = jnp.concatenate(
        [query_ref[:, head * HD:(head + 1) * HD] for head in range(group * heads, (group + 1) * heads)], axis=0
    )
    scores = lax.dot_general(stacked, keys, (((1,), (1,)), ((), ())), preferred_element_type=jnp.float32)
    peak = jnp.max(scores, axis=-1, keepdims=True)
    weights = jnp.exp2((scores - peak) * (LOG2E * HD ** -0.5))
    weight_ref[...] = weights.astype(jnp.bfloat16)
    inverse_ref[...] = 1.0 / jnp.sum(weights, axis=-1, keepdims=True)


def mix(weight_ref, inverse_ref, value_ref, value_part_ref, out_ref):
    count = out_ref.shape[0]
    values = summed(value_ref, value_part_ref).astype(jnp.bfloat16)
    numerator = jnp.dot(weight_ref[...], values, preferred_element_type=jnp.float32)
    attended = (numerator * inverse_ref[...]).astype(jnp.bfloat16)
    for head in range(out_ref.shape[1] // HD):
        out_ref[:, head * HD:(head + 1) * HD] = attended[head * count:(head + 1) * count]


def last_mix_kernel(weight_ref, inverse_ref, value_ref, value_part_ref, *rest):
    earlier, out_ref, stage, sem = rest[:-3], rest[-3], rest[-2], rest[-1]
    width = stage.shape[1]
    sources = (*earlier, stage)
    copies = [
        pltpu.make_async_copy(source, out_ref.at[:, group * width:(group + 1) * width], sem.at[group])
        for group, source in enumerate(sources)
    ]
    for copy in copies[:-1]:
        copy.start()
    mix(weight_ref, inverse_ref, value_ref, value_part_ref, stage)
    copies[-1].start()
    for copy in copies:
        copy.wait()


def local(queries, encoder_states, norm_gain, kv_weight, span_len, span_owner):
    sections, blocks, cores = (lax.axis_size(name) for name in ("section", "blk", "mp"))
    rows, features = encoder_states.shape
    depth = features // blocks
    local_groups = kv_weight.shape[3] // HD
    half = blocks // 2
    slots = MEAN * blocks
    query_rows, query_width = queries.shape[1:]
    core = lax.axis_index("mp")

    other_weight = lax.ppermute(kv_weight, "blk", [(b, (b + half) % blocks) for b in range(blocks)])
    outgoing = column_blocks(encoder_states, norm_gain, sections, blocks)
    own_rows = lax.all_to_all(outgoing, ("section", "blk"), 0, 0, tiled=True)
    other_rows = lax.ppermute(own_rows, "mp", [(c, (c + 1) % cores) for c in range(cores)])

    own_position = live_positions(span_len, span_owner, blocks, sections, cores, rows, core)
    other_position = live_positions(span_len, span_owner, blocks, sections, cores, rows, cores - 1 - core)
    outputs = pl.pallas_call(
        project_kernel,
        out_shape=(jax.ShapeDtypeStruct((slots, HD), jnp.float32),) * (2 * local_groups)
        + (jax.ShapeDtypeStruct((slots, 2 * HD), jnp.bfloat16),) * local_groups
        + (jax.ShapeDtypeStruct((slots, HD), jnp.bfloat16),) * local_groups,
        in_specs=[VMEM_SPEC] * 6,
        out_specs=(VMEM_SPEC,) * (4 * local_groups),
        compiler_params=GRANT,
        name="project",
    )(
        own_position,
        other_position,
        own_rows.reshape(-1, 2 * depth),
        other_rows.reshape(-1, 2 * depth),
        kv_weight[0].reshape(depth, -1),
        other_weight[0].reshape(depth, -1),
    )

    chains = 2 * local_groups
    sums, parts = list(outputs[:chains]), list(outputs[chains:])
    bits = [1 << place for place in range((half - 1).bit_length())]
    for step in range(len(bits)):
        for chain in range(chains):
            if step > 0:
                sums[chain], parts[chain] = add(sums[chain], parts[chain])
            bit = bits[(step + chain + 1) % len(bits)]
            parts[chain] = lax.ppermute(parts[chain], "blk", [(b, b ^ bit) for b in range(blocks)])

    group_shape = (query_rows, query_width // local_groups)
    group_heads = query_width // local_groups // HD
    scored = [
        pl.pallas_call(
            functools.partial(score_kernel, group),
            out_shape=(
                jax.ShapeDtypeStruct((group_heads * query_rows, slots), jnp.bfloat16),
                jax.ShapeDtypeStruct((group_heads * query_rows, 1), jnp.float32),
            ),
            in_specs=[VMEM_SPEC] * 3,
            out_specs=(VMEM_SPEC,) * 2,
            compiler_params=GRANT,
            name="score",
        )(queries[0], sums[group], parts[group])
        for group in range(local_groups)
    ]
    operands = [(*scored[group], sums[local_groups + group], parts[local_groups + group]) for group in range(local_groups)]
    attended = [
        pl.pallas_call(
            mix,
            out_shape=jax.ShapeDtypeStruct(group_shape, jnp.bfloat16),
            in_specs=[VMEM_SPEC] * 4,
            out_specs=VMEM_SPEC,
            compiler_params=GRANT,
            name="mix",
        )(*operands[group])
        for group in range(local_groups - 1)
    ]
    attended = pl.pallas_call(
        last_mix_kernel,
        out_shape=jax.ShapeDtypeStruct((query_rows, query_width), jnp.bfloat16),
        in_specs=[VMEM_SPEC] * (3 + local_groups),
        out_specs=ANY_SPEC,
        scratch_shapes=[pltpu.VMEM(group_shape, jnp.bfloat16), pltpu.SemaphoreType.DMA((local_groups,))],
        compiler_params=GRANT,
        name="mix_last",
    )(*operands[-1], *attended)
    return attended[None]


def solution(mesh):
    in_specs = (
        P("section", "blk", "mp"),
        P(("blk", "section", "mp"), None),
        P(),
        P("section", "blk", None, "mp"),
        P(),
        P(),
    )
    out_specs = P("section", "blk", "mp")
    return jax.shard_map(local, mesh=mesh, in_specs=in_specs, out_specs=out_specs, check_vma=False)
```
